128 devices in a mesh: row: 8 (over z_lo, x), col: 16 (over y, z_hi, core).
Axes of the slice: x: 4, y: 4, z: 4 (z_hi: 2, z_lo: 2; z = z_hi * 2 + z_lo), core: 2. Of those that a mesh axis runs over, the one named last changes fastest.
Arguments:
- amplitudes: bfloat16 [4096, 16384], P('row', 'col'), may hold values from -6 to 6
- integrals: bfloat16 [16384, 16384], P('col')
- block_irrep: int32 [64], replicated, may hold values from 0 to 3, as said below
- irrep_size: int32 [4], replicated, may hold values from 64 to 256
- partner: int32 [64], replicated, may hold values from 0 to 63, as said below
Outputs:
- residual: bfloat16 [4096, 16384], P('row', 'col')
The draws below stay inside these ranges and needn't reach their ends.
Inputs may be any that keep to these rules, and one draw needn't show every extreme that they name: partner is an involution on the 64 blocks without fixed blocks; a block and its partner have the same position among the 4 blocks of their col indices, and the blocks of one col index have partners at 4 different other col indices. `block_irrep`: a block and its partner have the same irrep.
All inputs are finite; a program needn't handle non-finite values.
Results may differ from the reference program's by a relative error of at most 0.0051.
Values may be sent and summed in bfloat16 or wider, within the bound.
A program may use at most 256 MiB of HBM per device.

```python
import jax
import jax.numpy as jnp
from jax import lax

BW = 256
NIRREP = 4
BPC = 4
NB = 64
K = 16384
NOCC = 64
OP = 4096


def partner_table(key):
    col_total = NB // BPC
    relabel = jax.random.permutation(jax.random.fold_in(key, 11), col_total).astype(jnp.int32)
    rounds = jax.random.permutation(jax.random.fold_in(key, 12), col_total - 1).astype(jnp.int32)[:BPC]
    inverse = jnp.zeros((col_total,), jnp.int32).at[relabel].set(jnp.arange(col_total, dtype=jnp.int32))
    blocks_all = jnp.arange(NB, dtype=jnp.int32)
    owner_col = blocks_all // BPC
    position = blocks_all % BPC
    round_pick = rounds[position]
    label_of = inverse[owner_col]
    mirror = jnp.mod(2 * round_pick - label_of, col_total - 1)
    matched = jnp.where(label_of == col_total - 1, round_pick, jnp.where(label_of == round_pick, col_total - 1, mirror))
    return (relabel[matched] * BPC + position).astype(jnp.int32)


def draw_partner(key, part):
    return partner_table(key)


def draw_block_irrep(key, part):
    matched = partner_table(key)
    blocks_all = jnp.arange(NB, dtype=jnp.int32)
    base_irrep = jax.random.randint(jax.random.fold_in(key, 13), (NB,), 0, NIRREP, dtype=jnp.int32)
    partner_zero = matched[0]
    spare_block = jnp.min(jnp.where((blocks_all != 0) & (blocks_all != partner_zero), blocks_all, NB))
    spare_low = jnp.minimum(spare_block, matched[spare_block])
    base_irrep = base_irrep.at[0].set(NIRREP - 1).at[spare_low].set(0)
    return base_irrep[jnp.minimum(blocks_all, matched)].astype(jnp.int32)


def draw_irrep_size(key, part):
    values = jax.random.randint(jax.random.fold_in(key, 21), (NIRREP,), BW // 4, BW + 1, dtype=jnp.int32)
    chosen = jax.random.randint(jax.random.fold_in(key, 22), (), 0, NIRREP, dtype=jnp.int32)
    slots_all = jnp.arange(NIRREP, dtype=jnp.int32)
    values = jnp.where(slots_all == chosen, BW, values)
    values = jnp.where(slots_all == (chosen + 1) % NIRREP, BW // 4, values)
    return values.astype(jnp.int32)


def draw_integrals(key, part):
    raw_draw = jax.random.normal(key, (K, K), jnp.float32)
    scaled = (raw_draw + raw_draw.T) * 0.5 ** 0.5 * (K / NIRREP) ** (-0.5)
    return scaled.astype(jnp.bfloat16)


def level_of(stream_key, shape, shards, low, top_value):
    loudness = 1.0
    for dim, blocks in shards:
        draws = jax.random.uniform(jax.random.fold_in(jax.random.fold_in(stream_key, 6), dim), (blocks,), jnp.float32, low / len(shards), top_value / len(shards))
        loudness = loudness * jnp.repeat(jnp.exp(draws), shape[dim] // blocks).reshape((-1,) + (1,) * (len(shape) - 1 - dim))
    return loudness


def centred(own_key, extent, spread, most, cuts=(), kind=jnp.bfloat16):
    array = jax.random.normal(own_key, extent, jnp.float32) * spread
    if len(cuts) > 0:
        array = level_of(own_key, extent, cuts, -0.22, 0.18) * array
    return jnp.clip(array, min=-most, max=most).astype(kind)


def setup_inputs(seed: int = 0) -> dict:
    key_of = jax.random.split(jax.random.key(seed), 6)
    amplitudes = centred(key_of[0], (OP, K), 1.0, 6.0, ((0, 8), (1, 16)))
    integrals = draw_integrals(jax.random.fold_in(key_of[5], 71), 0)
    block_irrep = draw_block_irrep(jax.random.fold_in(key_of[5], 71), 0)
    irrep_size = draw_irrep_size(jax.random.fold_in(key_of[5], 71), 0)
    partner = draw_partner(jax.random.fold_in(key_of[5], 71), 0)
    return dict(amplitudes=amplitudes, integrals=integrals, block_irrep=block_irrep, irrep_size=irrep_size, partner=partner)


def reference(amplitudes, integrals, block_irrep, irrep_size, partner):
    block_size = irrep_size[block_irrep]
    live_mask = (jnp.arange(BW, dtype=jnp.int32)[None, :] < block_size[:, None]).reshape(K)
    masked_amp = jnp.where(live_mask[None, :], amplitudes, jnp.zeros_like(amplitudes))

    def one_block(block_index):
        strip_rows = lax.dynamic_slice_in_dim(integrals, block_index * BW, BW, 0)
        own_irrep = lax.dynamic_index_in_dim(block_irrep, block_index, 0, keepdims=False)
        allowed = jnp.repeat(block_irrep == own_irrep, BW, total_repeat_length=K)
        strip_rows = jnp.where(allowed[None, :], strip_rows, jnp.zeros_like(strip_rows))
        return jnp.dot(masked_amp, strip_rows.T, preferred_element_type=jnp.float32).astype(jnp.bfloat16)

    pieces = lax.map(one_block, jnp.arange(NB, dtype=jnp.int32))
    ladder = jnp.transpose(pieces, (1, 0, 2)).reshape(OP, K)
    flipped = ladder.reshape(NOCC, NOCC, K).transpose(1, 0, 2).reshape(OP, K)
    fetched = jnp.take(flipped.reshape(OP, NB, BW), partner, axis=1).reshape(OP, K)
    combined = ladder.astype(jnp.float32) + fetched.astype(jnp.float32)
    return jnp.where(live_mask[None, :], combined, jnp.float32(0.0)).astype(jnp.bfloat16)
```

```python
import functools

import jax
import jax.numpy as jnp
from jax import lax
from jax.experimental import pallas as pl
from jax.experimental.pallas import tpu as pltpu
from jax.sharding import PartitionSpec as P

MESH = pl.DeviceIdType.MESH
BW = 256
BPC = 4
NOCC = 64
CHUNKS = 2
COLS = 16
ROWS = 8


def one_hot(shape, target):
    row = lax.broadcasted_iota(jnp.int32, shape, 0)
    column = lax.broadcasted_iota(jnp.int32, shape, 1)
    return jnp.where(column == target(row), 1.0, 0.0).astype(jnp.bfloat16)


def kernel(
    irrep, size, partner, amp_hbm, int_hbm, out_ref,
    amp, ints, own, total, ladder, send2, recv2,
    own_sem, int_sem, y_send, y_recv, k_send, k_recv, s1_send, s1_recv, s2_send, s2_recv, *recv1,
):
    rows = amp_hbm.shape[0]
    width = amp_hbm.shape[1]
    part = rows // CHUNKS
    firsts = ROWS // CHUNKS
    piece = part // COLS
    r, c = lax.axis_index("row"), lax.axis_index("col")
    y, zh, k = c // 4, (c // 2) % 2, c % 2

    def col(dy, dz, dk):
        return lax.rem(y + dy, 4) * 4 + lax.rem(zh + dz, 2) * 2 + lax.rem(k + dk, 2)

    up, down, across, twin = (r, col(1, 0, 0)), (r, col(3, 0, 0)), (r, col(0, 1, 0)), (r, col(0, 0, 1))

    own_copy = pltpu.make_async_copy(amp_hbm, own, own_sem)
    own_copy.start()

    barrier = pltpu.get_barrier_semaphore()

    def greet_col(o, carry):
        pl.semaphore_signal(barrier, inc=1, device_id=(r, lax.rem(c + o, COLS)), device_id_type=MESH)
        return carry

    lax.fori_loop(1, COLS, greet_col, 0)

    def group_at(row, s):
        sy, sz, sk = s // 4, (s // 2) % 2, s % 2
        x, z = lax.rem(row % 4 + sy + 2 * sk, 4), lax.rem(row // 4 + sz, 2)
        return (z * 4 + x) * 2 + sk

    def sender(row, slot):
        there, sk = slot // 2, slot % 2
        sz = lax.rem(row // 4 + there // 4, 2)
        sy = lax.rem(row % 4 + 8 - there % 4 - 2 * sk, 4)
        return there, sy * 4 + sz * 2 + sk

    target = group_at(r, c) // 2

    def greet_row(n, carry):
        there, column = sender(r, n)

        @pl.when(jnp.logical_or(there != r, column != c))
        def _():
            pl.semaphore_signal(barrier, inc=1, device_id=(there, column), device_id_type=MESH)

        return carry

    lax.fori_loop(0, 2 * ROWS, greet_row, 0)

    def int_copy(n):
        at = lax.rem(c + n, COLS)
        return pltpu.make_async_copy(
            int_hbm.at[:, pl.ds(pl.multiple_of(at * width, width), width)], ints.at[at], int_sem.at[at]
        )

    def start_int(n, carry):
        int_copy(n).start()
        return carry

    lax.fori_loop(0, COLS, start_int, 0)

    def live_of(base):
        lane = lax.broadcasted_iota(jnp.int32, (1, BW), 1)
        return jnp.concatenate(
            [jnp.where(lane < size[irrep[base + b]], 1.0, 0.0) for b in range(BPC)], axis=1
        )

    live = live_of(c * BPC)

    def natural(n):
        group, rest = n // piece, n % piece
        return (rest // 4) * NOCC + group * 4 + rest % 4

    own_copy.wait()
    arrange = one_hot((part, part), natural)
    for q in range(CHUNKS):
        rearranged = jnp.dot(arrange, own[q * part : (q + 1) * part, :], preferred_element_type=jnp.float32)
        amp[c, q * part : (q + 1) * part, :] = (rearranged * live).astype(jnp.bfloat16)

    pl.semaphore_wait(barrier, COLS - 1 + jnp.where(target == r, 2 * ROWS - 1, 2 * ROWS))

    def move(at, q, start, count, to, sems, n):
        span = pl.ds(q * part + start, count)
        return pltpu.make_async_remote_copy(
            src_ref=amp.at[at, span], dst_ref=amp.at[at, span],
            send_sem=sems[0].at[q, n], recv_sem=sems[1].at[q, n],
            device_id=to, device_id_type=MESH,
        )

    half = part // 2
    ysem, ksem = (y_send, y_recv), (k_send, k_recv)
    started = []

    def go(copy):
        copy.start()
        started.append(copy)

    def send_own(q):
        go(move(c, q, 0, part, up, ysem, 0))
        go(move(c, q, 0, part, down, ysem, 1))
        go(move(c, q, 0, part, across, ysem, 4))
        go(move(c, q, 0, part, twin, ksem, 0))

    def arrived(at, q, start, count, sems, n):
        move(at, q, start, count, up, sems, n).wait_recv()

    def near(q):
        at = col(3, 0, 0)
        arrived(at, q, 0, part, ysem, 0)
        go(move(at, q, 0, half, up, ysem, 2))
        go(move(at, q, 0, part, twin, ksem, 1))
        at = col(1, 0, 0)
        arrived(at, q, 0, part, ysem, 1)
        go(move(at, q, half, half, down, ysem, 3))
        go(move(at, q, 0, part, twin, ksem, 2))

    def over(q):
        at = col(0, 1, 0)
        arrived(at, q, 0, part, ysem, 4)
        go(move(at, q, 0, part, up, ysem, 5))
        go(move(at, q, 0, part, down, ysem, 6))
        go(move(at, q, 0, part, twin, ksem, 3))

    def far(q):
        at = col(2, 0, 0)
        arrived(at, q, 0, half, ysem, 2)
        go(move(at, q, 0, half, across, ysem, 7))
        arrived(at, q, half, half, ysem, 3)
        go(move(at, q, half, half, across, ysem, 8))
        go(move(at, q, 0, part, twin, ksem, 4))

    def near_over(q):
        at = col(3, 1, 0)
        arrived(at, q, 0, part, ysem, 5)
        go(move(at, q, 0, part, twin, ksem, 5))
        at = col(1, 1, 0)
        arrived(at, q, 0, part, ysem, 6)
        go(move(at, q, 0, part, twin, ksem, 6))

    def far_over(q):
        at = col(2, 1, 0)
        arrived(at, q, 0, half, ysem, 7)
        arrived(at, q, half, half, ysem, 8)
        go(move(at, q, 0, part, twin, ksem, 7))

    def mask_ints(n, carry):
        int_copy(n).wait()
        at = lax.rem(c + n, COLS)
        for a in range(BPC):
            for b in range(BPC):
                same = irrep[c * BPC + a] == irrep[at * BPC + b]
                keep = jnp.where(same, 1.0, 0.0).astype(jnp.bfloat16)
                ints[at, a * BW : (a + 1) * BW, b * BW : (b + 1) * BW] *= keep
        return carry

    def multiply(q, at, first=False):
        def block(a, carry):
            span = pl.ds(pl.multiple_of(a * BW, BW), BW)
            product = lax.dot_general(
                amp[at, q * part : (q + 1) * part, :], ints[at, span, :],
                (((1,), (1,)), ((), ())), preferred_element_type=jnp.float32,
            )
            total[q, a] = product if first else total[q, a] + product
            return carry

        lax.fori_loop(0, BPC, block, 0)

    def from_twin(q, n):
        dy, dz = ((0, 0), (3, 0), (1, 0), (0, 1), (2, 0), (3, 1), (1, 1), (2, 1))[n]
        at = col(dy, dz, 1)
        arrived(at, q, 0, part, ksem, n)
        multiply(q, at)

    def step1(q, o):
        to = lax.rem(c + o, COLS)
        return pltpu.make_async_remote_copy(
            src_ref=ladder.at[q, group_at(r, to)], dst_ref=recv1[q].at[c], send_sem=s1_send.at[q, to], recv_sem=s1_recv.at[q, c],
            device_id=(r, to), device_id_type=MESH,
        )

    def exchange1(q):
        for a in range(BPC):
            ladder[q, :, :, a * BW : (a + 1) * BW] = total[q, a].astype(jnp.bfloat16).reshape(COLS, piece, BW)

        def send(o, carry):
            step1(q, o).start()
            return carry

        lax.fori_loop(1, COLS, send, 0)
        recv1[q][c] = ladder[q, group_at(r, c)]

    def step2(q, to, slot):
        return pltpu.make_async_remote_copy(
            src_ref=send2.at[q, to], dst_ref=recv2.at[q, slot], send_sem=s2_send.at[q, to], recv_sem=s2_recv.at[q, slot],
            device_id=(target, to), device_id_type=MESH,
        )

    mine = r * 2 + k

    def exchange2(q):
        def arrive(o, carry):
            at = lax.rem(c + o, COLS)
            pltpu.make_async_remote_copy(
                src_ref=ladder.at[q, at], dst_ref=recv1[q].at[at], send_sem=s1_send.at[q, at], recv_sem=s1_recv.at[q, at],
                device_id=(r, at), device_id_type=MESH,
            ).wait_recv()
            return carry

        lax.fori_loop(1, COLS, arrive, 0)

        def send(o, carry):
            to = lax.rem(c + o, COLS)
            for b in range(BPC):
                source = partner[to * BPC + b] // BPC
                send2[q, to, :, b * BW : (b + 1) * BW] = recv1[q][source, :, b * BW : (b + 1) * BW]

            local = jnp.logical_and(target == r, to == c)

            @pl.when(jnp.logical_not(local))
            def _():
                step2(q, to, mine).start()

            @pl.when(local)
            def _():
                recv2[q, mine] = send2[q, to]

            return carry

        lax.fori_loop(0, COLS, send, 0)

    def exchange2_done(q):
        def arrive(slot, carry):
            there, column = sender(r, slot)

            @pl.when(jnp.logical_or(there != r, column != c))
            def _():
                step2(q, c, slot).wait_recv()

            return carry

        lax.fori_loop(0, 2 * ROWS, arrive, 0)

    def unnatural(m):
        first, second = m // NOCC, m % NOCC
        return (second // 4) * piece + first * 4 + second % 4

    for q in range(CHUNKS):
        send_own(q)
    lax.fori_loop(0, COLS, mask_ints, 0)
    for q in range(CHUNKS):
        multiply(q, c, first=True)
    for q in range(CHUNKS):
        near(q)
        over(q)
        from_twin(q, 0)
    far(0)
    far(1)
    for q in range(CHUNKS):
        multiply(q, col(3, 0, 0))
        multiply(q, col(1, 0, 0))
        multiply(q, col(0, 1, 0))
        from_twin(q, 1)
        from_twin(q, 2)
        from_twin(q, 3)
        multiply(q, col(2, 0, 0))
    near_over(0)
    from_twin(0, 4)
    multiply(0, col(3, 1, 0))
    multiply(0, col(1, 1, 0))
    far_over(0)
    from_twin(0, 5)
    from_twin(0, 6)
    multiply(0, col(2, 1, 0))
    near_over(1)
    from_twin(0, 7)
    exchange1(0)
    from_twin(1, 4)
    multiply(1, col(3, 1, 0))
    multiply(1, col(1, 1, 0))
    far_over(1)
    from_twin(1, 5)
    from_twin(1, 6)
    multiply(1, col(2, 1, 0))
    from_twin(1, 7)
    exchange1(1)
    exchange2(0)
    exchange2(1)
    for q in range(CHUNKS):
        exchange2_done(q)

    back = one_hot((part, part), unnatural)
    for q in range(CHUNKS):
        result = jnp.dot(back, ladder[q].reshape(part, width), preferred_element_type=jnp.float32)
        for p in range(CHUNKS):
            row = lax.broadcasted_iota(jnp.int32, (part, part), 0)
            column = lax.broadcasted_iota(jnp.int32, (part, part), 1)
            slot, rest = column // piece, column % piece
            first = (slot % 2) * 4 + rest % 4
            second = (slot // 2) * ROWS + p * firsts + rest // 4
            fetch = jnp.where(first * NOCC + second == row + q * part, 1.0, 0.0).astype(jnp.bfloat16)
            result += jnp.dot(fetch, recv2[p].reshape(part, width), preferred_element_type=jnp.float32)
        out_ref[q * part : (q + 1) * part, :] = (result * live).astype(jnp.bfloat16)

    for copy in started:
        copy.wait_send()
    for q in range(CHUNKS):

        def sent1(o, carry):
            step1(q, o).wait_send()
            return carry

        lax.fori_loop(1, COLS, sent1, 0)

        def sent2(to, carry):
            @pl.when(jnp.logical_not(jnp.logical_and(target == r, to == c)))
            def _():
                step2(q, to, mine).wait_send()

            return carry

        lax.fori_loop(0, COLS, sent2, 0)


def body(amplitudes, integrals, block_irrep, irrep_size, partner):
    rows, width = amplitudes.shape
    part = rows // CHUNKS
    piece = part // COLS
    dma = pltpu.SemaphoreType.DMA
    return pl.pallas_call(
        kernel,
        out_shape=jax.ShapeDtypeStruct((rows, width), jnp.bfloat16),
        in_specs=[pl.BlockSpec(memory_space=pltpu.SMEM)] * 3 + [pl.BlockSpec(memory_space=pl.ANY)] * 2,
        out_specs=pl.BlockSpec(memory_space=pltpu.VMEM),
        scratch_shapes=[
            pltpu.VMEM((COLS, rows, width), jnp.bfloat16),
            pltpu.VMEM((COLS, width, width), jnp.bfloat16),
            pltpu.VMEM((rows, width), jnp.bfloat16),
            pltpu.VMEM((CHUNKS, BPC, part, BW), jnp.float32),
            pltpu.VMEM((CHUNKS, COLS, piece, width), jnp.bfloat16),
            pltpu.VMEM((CHUNKS, COLS, piece, width), jnp.bfloat16),
            pltpu.VMEM((CHUNKS, COLS, piece, width), jnp.bfloat16),
            dma,
            dma((COLS,)),
            dma((CHUNKS, 9)),
            dma((CHUNKS, 9)),
            dma((CHUNKS, 8)),
            dma((CHUNKS, 8)),
            dma((CHUNKS, COLS)),
            dma((CHUNKS, COLS)),
            dma((CHUNKS, COLS)),
            dma((CHUNKS, COLS)),
        ]
        + [pltpu.VMEM((COLS, piece, width), jnp.bfloat16)] * CHUNKS,
        compiler_params=pltpu.CompilerParams(
            collective_id=0, has_side_effects=True, vmem_limit_bytes=60 * 2**20
        ),
        name="ladder",
    )(block_irrep, irrep_size, partner, amplitudes, integrals)


def solution(mesh):
    in_specs = (P("row", "col"), P("col", None), P(), P(), P())
    return jax.shard_map(body, mesh=mesh, in_specs=in_specs, out_specs=P("row", "col"), check_vma=False)
```

```python
import jax
import jax.numpy as jnp
from jax import lax
from jax.experimental import pallas as pl
from jax.experimental.pallas import tpu as pltpu
from jax.sharding import PartitionSpec as P

MESH = pl.DeviceIdType.MESH
BW = 256
BPC = 4
NOCC = 64
COLS = 16
ROWS = 8
FIRSTS = (4, 4)
CHUNKS = len(FIRSTS)


def one_hot(shape, target):
    row = lax.broadcasted_iota(jnp.int32, shape, 0)
    column = lax.broadcasted_iota(jnp.int32, shape, 1)
    return jnp.where(column == target(row), 1.0, 0.0).astype(jnp.bfloat16)


def kernel(irrep, size, partner, amp_hbm, int_hbm, out_ref, *scratch):
    (amp, ints, own, own_sem, int_sem, y_send, y_recv, k_send, k_recv, s1_send, s1_recv, s2_send, s2_recv, ready) = scratch[:14]
    total, ladder, recv1, send2, recv2 = (scratch[14 + n * CHUNKS : 14 + (n + 1) * CHUNKS] for n in range(5))
    rows, width = amp_hbm.shape
    parts = [f * NOCC for f in FIRSTS]
    begins = [sum(parts[:q]) for q in range(CHUNKS)]
    pieces = [p // COLS for p in parts]
    r, c = lax.axis_index("row"), lax.axis_index("col")
    y, zh, k = c // 4, (c // 2) % 2, c % 2

    def col(dy, dz, dk):
        return lax.rem(y + dy, 4) * 4 + lax.rem(zh + dz, 2) * 2 + lax.rem(k + dk, 2)

    up, down, across, twin = (r, col(1, 0, 0)), (r, col(3, 0, 0)), (r, col(0, 1, 0)), (r, col(0, 0, 1))

    def group_at(row, s):
        sy, sz, sk = s // 4, (s // 2) % 2, s % 2
        x, z = lax.rem(row % 4 + sy + 2 * sk, 4), lax.rem(row // 4 + sz, 2)
        return (z * 4 + x) * 2 + sk

    def sender(row, slot):
        there, sk = slot // 2, slot % 2
        sz = lax.rem(row // 4 + there // 4, 2)
        sy = lax.rem(row % 4 + 8 - there % 4 - 2 * sk, 4)
        return there, sy * 4 + sz * 2 + sk

    target = group_at(r, c) // 2
    origin = lax.rem(r // 4 + zh, 2) * 4 + lax.rem(r % 4 + 8 - y - 2 * k, 4)
    moves = target != r

    own_copy = pltpu.make_async_copy(amp_hbm, own, own_sem)
    own_copy.start()

    barrier = pltpu.get_barrier_semaphore()
    for to in (up, down, across, twin):
        pl.semaphore_signal(barrier, inc=1, device_id=to, device_id_type=MESH)

    @pl.when(moves)
    def _():
        pl.semaphore_signal(barrier, inc=1, device_id=(target, c), device_id_type=MESH)

    def int_copy(n):
        at = lax.rem(c + n, COLS)
        return pltpu.make_async_copy(
            int_hbm.at[:, pl.ds(pl.multiple_of(at * width, width), width)], ints.at[at], int_sem.at[at]
        )

    def live_of(base):
        lane = lax.broadcasted_iota(jnp.int32, (1, BW), 1)
        return jnp.concatenate(
            [jnp.where(lane < size[irrep[base + b]], 1.0, 0.0) for b in range(BPC)], axis=1
        )

    live = live_of(c * BPC)

    own_copy.wait()
    amp[c] = own[...] * live.astype(jnp.bfloat16)

    def start_int(n, carry):
        int_copy(n).start()
        return carry

    pl.semaphore_wait(barrier, jnp.where(moves, 5, 4))

    def move(at, q, start, count, to, sems, n):
        span = pl.ds(begins[q] + start, count)
        return pltpu.make_async_remote_copy(
            src_ref=amp.at[at, span], dst_ref=amp.at[at, span],
            send_sem=sems[0].at[q, n], recv_sem=sems[1].at[q, n],
            device_id=to, device_id_type=MESH,
        )

    ysem, ksem = (y_send, y_recv), (k_send, k_recv)
    started = []

    def go(copy):
        copy.start()
        started.append(copy)

    def send_own(q):
        go(move(c, q, 0, parts[q], up, ysem, 0))
        go(move(c, q, 0, parts[q], down, ysem, 1))
        go(move(c, q, 0, parts[q], across, ysem, 4))
        go(move(c, q, 0, parts[q], twin, ksem, 0))

    def arrived(at, q, start, count, sems, n):
        move(at, q, start, count, up, sems, n).wait_recv()

    def near(q):
        half = parts[q] // 2
        at = col(3, 0, 0)
        arrived(at, q, 0, parts[q], ysem, 0)
        go(move(at, q, 0, half, up, ysem, 2))
        go(move(at, q, half, half, across, ysem, 7))
        at = col(1, 0, 0)
        arrived(at, q, 0, parts[q], ysem, 1)
        go(move(at, q, half, half, down, ysem, 3))
        go(move(at, q, 0, half, across, ysem, 8))

    def near_twin(q):
        go(move(col(3, 0, 0), q, 0, parts[q], twin, ksem, 1))
        go(move(col(1, 0, 0), q, 0, parts[q], twin, ksem, 2))

    def over(q):
        half = parts[q] // 2
        at = col(0, 1, 0)
        arrived(at, q, 0, parts[q], ysem, 4)
        go(move(at, q, 0, half, up, ysem, 5))
        go(move(at, q, half, half, down, ysem, 6))
        go(move(at, q, 0, parts[q], twin, ksem, 3))

    def far(q):
        half = parts[q] // 2
        at = col(2, 0, 0)
        arrived(at, q, 0, half, ysem, 2)
        arrived(at, q, half, half, ysem, 3)
        go(move(at, q, 0, parts[q], twin, ksem, 4))

    def near_over(q):
        half = parts[q] // 2
        at = col(3, 1, 0)
        arrived(at, q, 0, half, ysem, 5)
        go(move(at, q, 0, half, up, ysem, 9))
        at = col(1, 1, 0)
        arrived(at, q, half, half, ysem, 6)
        go(move(at, q, half, half, down, ysem, 10))

    def near_over_twin(q):
        half = parts[q] // 2
        at = col(3, 1, 0)
        arrived(at, q, half, half, ysem, 7)
        go(move(at, q, 0, parts[q], twin, ksem, 5))
        at = col(1, 1, 0)
        arrived(at, q, 0, half, ysem, 8)
        go(move(at, q, 0, parts[q], twin, ksem, 6))

    def far_over(q):
        half = parts[q] // 2
        at = col(2, 1, 0)
        arrived(at, q, 0, half, ysem, 9)
        arrived(at, q, half, half, ysem, 10)
        go(move(at, q, 0, parts[q], twin, ksem, 7))

    def mask_ints(n, carry):
        int_copy(n).wait()
        at = lax.rem(c + n, COLS)
        for a in range(BPC):
            for b in range(BPC):
                same = irrep[c * BPC + a] == irrep[at * BPC + b]
                keep = jnp.where(same, 1.0, 0.0).astype(jnp.bfloat16)
                ints[at, a * BW : (a + 1) * BW, b * BW : (b + 1) * BW] *= keep
        return carry

    def multiply(q, at, first=False):
        product = lax.dot_general(
            ints[at], amp[at, begins[q] : begins[q] + parts[q], :],
            (((1,), (1,)), ((), ())), preferred_element_type=jnp.float32,
        )
        total[q][...] = product if first else total[q][...] + product

    def from_twin(q, n):
        dy, dz = ((0, 0), (3, 0), (1, 0), (0, 1), (2, 0), (3, 1), (1, 1), (2, 1))[n]
        at = col(dy, dz, 1)
        arrived(at, q, 0, parts[q], ksem, n)
        multiply(q, at)

    def row_ready():
        @pl.when(moves)
        def _():
            pl.semaphore_signal(ready, inc=1, device_id=(origin, c), device_id_type=MESH)

    def target_ready():
        @pl.when(moves)
        def _():
            pl.semaphore_wait(ready, 1)

    def step1(q, o):
        to = lax.rem(c + o, COLS)
        return pltpu.make_async_remote_copy(
            src_ref=ladder[q].at[group_at(r, to)], dst_ref=recv1[q].at[c], send_sem=s1_send.at[q, to], recv_sem=s1_recv.at[q, c],
            device_id=(r, to), device_id_type=MESH,
        )

    def exchange1(q):
        piece = pieces[q]

        def natural(n):
            group, rest = n // piece, n % piece
            return (rest // 4) * NOCC + group * 4 + rest % 4

        turned = lax.dot_general(
            one_hot((parts[q], parts[q]), natural), total[q][...].astype(jnp.bfloat16),
            (((1,), (1,)), ((), ())), preferred_element_type=jnp.float32,
        )
        ladder[q][...] = turned.astype(jnp.bfloat16).reshape(COLS, piece, width)

        def send(o, carry):
            step1(q, o).start()
            return carry

        lax.fori_loop(1, COLS, send, 0)
        recv1[q][c] = ladder[q][group_at(r, c)]

    def step2(q, to, slot):
        return pltpu.make_async_remote_copy(
            src_ref=send2[q].at[to], dst_ref=recv2[q].at[slot], send_sem=s2_send.at[q, to], recv_sem=s2_recv.at[q, slot],
            device_id=(target, to), device_id_type=MESH,
        )

    mine = r * 2 + k

    def exchange2(q):
        def arrive(o, carry):
            at = lax.rem(c + o, COLS)
            pltpu.make_async_remote_copy(
                src_ref=ladder[q].at[at], dst_ref=recv1[q].at[at], send_sem=s1_send.at[q, at], recv_sem=s1_recv.at[q, at],
                device_id=(r, at), device_id_type=MESH,
            ).wait_recv()
            return carry

        lax.fori_loop(1, COLS, arrive, 0)

        def send(o, carry):
            to = lax.rem(c + o, COLS)
            for b in range(BPC):
                source = partner[to * BPC + b] // BPC
                send2[q][to, :, b * BW : (b + 1) * BW] = recv1[q][source, :, b * BW : (b + 1) * BW]

            local = jnp.logical_and(target == r, to == c)

            @pl.when(jnp.logical_not(local))
            def _():
                step2(q, to, mine).start()

            @pl.when(local)
            def _():
                recv2[q][mine] = send2[q][to]

            return carry

        lax.fori_loop(0, COLS, send, 0)

    def exchange2_done(q):
        def arrive(slot, carry):
            there, column = sender(r, slot)

            @pl.when(jnp.logical_or(there != r, column != c))
            def _():
                step2(q, c, slot).wait_recv()

            return carry

        lax.fori_loop(0, 2 * ROWS, arrive, 0)

    send_own(0)
    lax.fori_loop(0, COLS, start_int, 0)
    lax.fori_loop(0, COLS, mask_ints, 0)
    multiply(0, c, first=True)
    near(0)
    over(0)
    send_own(1)
    near_twin(0)
    multiply(1, c, first=True)
    from_twin(0, 0)
    multiply(0, col(3, 0, 0))
    multiply(0, col(1, 0, 0))
    multiply(0, col(0, 1, 0))
    from_twin(0, 1)
    near_over(0)
    far(0)
    from_twin(0, 2)
    from_twin(0, 3)
    near(1)
    over(1)
    near_twin(1)
    near_over_twin(0)
    multiply(0, col(2, 0, 0))
    from_twin(0, 4)
    multiply(0, col(3, 1, 0))
    multiply(0, col(1, 1, 0))
    far_over(0)
    from_twin(0, 5)
    from_twin(0, 6)
    multiply(0, col(2, 1, 0))
    from_twin(0, 7)
    row_ready()
    exchange1(0)
    from_twin(1, 0)
    multiply(1, col(3, 0, 0))
    multiply(1, col(1, 0, 0))
    near_over(1)
    multiply(1, col(0, 1, 0))
    far(1)
    from_twin(1, 1)
    from_twin(1, 2)
    from_twin(1, 3)
    target_ready()
    exchange2(0)
    near_over_twin(1)
    multiply(1, col(2, 0, 0))
    from_twin(1, 4)
    multiply(1, col(3, 1, 0))
    multiply(1, col(1, 1, 0))
    far_over(1)
    from_twin(1, 5)
    from_twin(1, 6)
    multiply(1, col(2, 1, 0))
    from_twin(1, 7)
    exchange1(1)
    exchange2(1)
    exchange2_done(0)
    exchange2_done(1)
    for q in range(CHUNKS):
        piece = pieces[q]

        def grouped(m):
            first, second = m // NOCC, m % NOCC
            return (second // 4) * piece + first * 4 + second % 4

        result = jnp.dot(
            one_hot((parts[q], parts[q]), grouped), ladder[q][...].reshape(parts[q], width), preferred_element_type=jnp.float32
        )
        for p in range(CHUNKS):
            row = lax.broadcasted_iota(jnp.int32, (parts[q], parts[p]), 0)
            column = lax.broadcasted_iota(jnp.int32, (parts[q], parts[p]), 1)
            slot, rest = column // pieces[p], column % pieces[p]
            first = (slot % 2) * 4 + rest % 4
            second = (slot // 2) * ROWS + begins[p] // NOCC + rest // 4
            fetch = jnp.where(first * NOCC + second == row + begins[q], 1.0, 0.0).astype(jnp.bfloat16)
            result += jnp.dot(fetch, recv2[p][...].reshape(parts[p], width), preferred_element_type=jnp.float32)
        out_ref[begins[q] : begins[q] + parts[q], :] = (result * live).astype(jnp.bfloat16)

    for copy in started:
        copy.wait_send()
    for q in range(CHUNKS):

        def sent1(o, carry):
            step1(q, o).wait_send()
            return carry

        lax.fori_loop(1, COLS, sent1, 0)

        def sent2(to, carry):
            @pl.when(jnp.logical_not(jnp.logical_and(target == r, to == c)))
            def _():
                step2(q, to, mine).wait_send()

            return carry

        lax.fori_loop(0, COLS, sent2, 0)


def body(amplitudes, integrals, block_irrep, irrep_size, partner):
    rows, width = amplitudes.shape
    dma = pltpu.SemaphoreType.DMA
    held = [pltpu.VMEM((COLS, f * NOCC // COLS, width), jnp.bfloat16) for f in FIRSTS]
    return pl.pallas_call(
        kernel,
        out_shape=jax.ShapeDtypeStruct((rows, width), jnp.bfloat16),
        in_specs=[pl.BlockSpec(memory_space=pltpu.SMEM)] * 3 + [pl.BlockSpec(memory_space=pl.ANY)] * 2,
        out_specs=pl.BlockSpec(memory_space=pltpu.VMEM),
        scratch_shapes=[
            pltpu.VMEM((COLS, rows, width), jnp.bfloat16),
            pltpu.VMEM((COLS, width, width), jnp.bfloat16),
            pltpu.VMEM((rows, width), jnp.bfloat16),
            dma,
            dma((COLS,)),
            dma((CHUNKS, 11)),
            dma((CHUNKS, 11)),
            dma((CHUNKS, 8)),
            dma((CHUNKS, 8)),
            dma((CHUNKS, COLS)),
            dma((CHUNKS, COLS)),
            dma((CHUNKS, COLS)),
            dma((CHUNKS, COLS)),
            pltpu.SemaphoreType.REGULAR,
        ]
        + [pltpu.VMEM((width, f * NOCC), jnp.float32) for f in FIRSTS]
        + held * 4,
        compiler_params=pltpu.CompilerParams(
            collective_id=0, has_side_effects=True, vmem_limit_bytes=58 * 2**20
        ),
        name="ladder",
    )(block_irrep, irrep_size, partner, amplitudes, integrals)


def solution(mesh):
    in_specs = (P("row", "col"), P("col", None), P(), P(), P())
    return jax.shard_map(body, mesh=mesh, in_specs=in_specs, out_specs=P("row", "col"), check_vma=False)
```

```python
import jax
import jax.numpy as jnp
from jax import lax
from jax.experimental import pallas as pl
from jax.experimental.pallas import tpu as pltpu
from jax.sharding import PartitionSpec as P

MESH = pl.DeviceIdType.MESH
BW = 256
BPC = 4
NOCC = 64
COLS = 16
ROWS = 8
FIRSTS = (4, 4)
CHUNKS = len(FIRSTS)


def one_hot(shape, target):
    row = lax.broadcasted_iota(jnp.int32, shape, 0)
    column = lax.broadcasted_iota(jnp.int32, shape, 1)
    return jnp.where(column == target(row), 1.0, 0.0).astype(jnp.bfloat16)


def kernel(irrep, size, partner, amp_hbm, int_hbm, out_ref, *scratch):
    (amp, ints, own_sem, int_sem, y_send, y_recv, k_send, k_recv, s1_send, s1_recv, s2_send, s2_recv, ready) = scratch[:13]
    total, ladder, recv1, send2, recv2 = (scratch[13 + n * CHUNKS : 13 + (n + 1) * CHUNKS] for n in range(5))
    rows, width = amp_hbm.shape
    parts = [f * NOCC for f in FIRSTS]
    begins = [sum(parts[:q]) for q in range(CHUNKS)]
    pieces = [p // COLS for p in parts]
    r, c = lax.axis_index("row"), lax.axis_index("col")
    y, zh, k = c // 4, (c // 2) % 2, c % 2

    def col(dy, dz, dk):
        return lax.rem(y + dy, 4) * 4 + lax.rem(zh + dz, 2) * 2 + lax.rem(k + dk, 2)

    up, down, across, twin = (r, col(1, 0, 0)), (r, col(3, 0, 0)), (r, col(0, 1, 0)), (r, col(0, 0, 1))

    def group_at(row, s):
        sy, sz, sk = s // 4, (s // 2) % 2, s % 2
        x, z = lax.rem(row % 4 + sy + 2 * sk, 4), lax.rem(row // 4 + sz, 2)
        return (z * 4 + x) * 2 + sk

    def sender(row, slot):
        there, sk = slot // 2, slot % 2
        sz = lax.rem(row // 4 + there // 4, 2)
        sy = lax.rem(row % 4 + 8 - there % 4 - 2 * sk, 4)
        return there, sy * 4 + sz * 2 + sk

    target = group_at(r, c) // 2
    origin = lax.rem(r // 4 + zh, 2) * 4 + lax.rem(r % 4 + 8 - y - 2 * k, 4)
    moves = target != r

    own_copy = pltpu.make_async_copy(amp_hbm, amp.at[c], own_sem)
    own_copy.start()

    barrier = pltpu.get_barrier_semaphore()
    for to in (up, down, across, twin):
        pl.semaphore_signal(barrier, inc=1, device_id=to, device_id_type=MESH)

    @pl.when(moves)
    def _():
        pl.semaphore_signal(barrier, inc=1, device_id=(target, c), device_id_type=MESH)

    def int_copy(n):
        at = lax.rem(c + n, COLS)
        return pltpu.make_async_copy(
            int_hbm.at[:, pl.ds(pl.multiple_of(at * width, width), width)], ints.at[at], int_sem.at[at]
        )

    def live_of(base):
        lane = lax.broadcasted_iota(jnp.int32, (1, BW), 1)
        return jnp.concatenate(
            [jnp.where(lane < size[irrep[base + b]], 1.0, 0.0) for b in range(BPC)], axis=1
        )

    live = live_of(c * BPC)

    own_copy.wait()
    amp[c] *= live.astype(jnp.bfloat16)

    def start_int(n, carry):
        int_copy(n).start()
        return carry

    pl.semaphore_wait(barrier, jnp.where(moves, 5, 4))

    def move(at, q, start, count, to, sems, n):
        span = pl.ds(begins[q] + start, count)
        return pltpu.make_async_remote_copy(
            src_ref=amp.at[at, span], dst_ref=amp.at[at, span],
            send_sem=sems[0].at[q, n], recv_sem=sems[1].at[q, n],
            device_id=to, device_id_type=MESH,
        )

    ysem, ksem = (y_send, y_recv), (k_send, k_recv)
    started = []

    def go(copy):
        copy.start()
        started.append(copy)

    def send_own(q):
        go(move(c, q, 0, parts[q], up, ysem, 0))
        go(move(c, q, 0, parts[q], down, ysem, 1))
        go(move(c, q, 0, parts[q], across, ysem, 4))
        go(move(c, q, 0, parts[q], twin, ksem, 0))

    def arrived(at, q, start, count, sems, n):
        move(at, q, start, count, up, sems, n).wait_recv()

    def near(q):
        half = parts[q] // 2
        at = col(3, 0, 0)
        arrived(at, q, 0, parts[q], ysem, 0)
        go(move(at, q, 0, half, up, ysem, 2))
        go(move(at, q, half, half, across, ysem, 7))
        at = col(1, 0, 0)
        arrived(at, q, 0, parts[q], ysem, 1)
        go(move(at, q, half, half, down, ysem, 3))
        go(move(at, q, 0, half, across, ysem, 8))

    def near_twin(q):
        go(move(col(3, 0, 0), q, 0, parts[q], twin, ksem, 1))
        go(move(col(1, 0, 0), q, 0, parts[q], twin, ksem, 2))

    def over(q):
        half = parts[q] // 2
        at = col(0, 1, 0)
        arrived(at, q, 0, parts[q], ysem, 4)
        go(move(at, q, 0, half, up, ysem, 5))
        go(move(at, q, half, half, down, ysem, 6))
        go(move(at, q, 0, parts[q], twin, ksem, 3))

    def edge(q):
        return parts[q] * 5 // 16

    def far(q):
        half = parts[q] // 2
        at = col(2, 0, 0)
        arrived(at, q, 0, half, ysem, 2)
        arrived(at, q, half, half, ysem, 3)
        go(move(at, q, edge(q), parts[q] - 2 * edge(q), across, ysem, 11))
        go(move(at, q, 0, parts[q], twin, ksem, 4))

    def near_over(q):
        half = parts[q] // 2
        at = col(3, 1, 0)
        arrived(at, q, 0, half, ysem, 5)
        go(move(at, q, 0, edge(q), up, ysem, 9))
        at = col(1, 1, 0)
        arrived(at, q, half, half, ysem, 6)
        go(move(at, q, parts[q] - edge(q), edge(q), down, ysem, 10))

    def near_over_twin(q):
        half = parts[q] // 2
        at = col(3, 1, 0)
        arrived(at, q, half, half, ysem, 7)
        go(move(at, q, 0, parts[q], twin, ksem, 5))
        at = col(1, 1, 0)
        arrived(at, q, 0, half, ysem, 8)
        go(move(at, q, 0, parts[q], twin, ksem, 6))

    def far_over(q):
        at = col(2, 1, 0)
        arrived(at, q, 0, edge(q), ysem, 9)
        arrived(at, q, parts[q] - edge(q), edge(q), ysem, 10)
        arrived(at, q, edge(q), parts[q] - 2 * edge(q), ysem, 11)
        go(move(at, q, 0, parts[q], twin, ksem, 7))

    def mask_ints(n, carry):
        int_copy(n).wait()
        at = lax.rem(c + n, COLS)
        for a in range(BPC):
            for b in range(BPC):
                same = irrep[c * BPC + a] == irrep[at * BPC + b]
                keep = jnp.where(same, 1.0, 0.0).astype(jnp.bfloat16)
                ints[at, a * BW : (a + 1) * BW, b * BW : (b + 1) * BW] *= keep
        return carry

    def multiply(q, at, first=False):
        product = lax.dot_general(
            ints[at], amp[at, begins[q] : begins[q] + parts[q], :],
            (((1,), (1,)), ((), ())), preferred_element_type=jnp.float32,
        )
        total[q][...] = product if first else total[q][...] + product

    def from_twin(q, n):
        dy, dz = ((0, 0), (3, 0), (1, 0), (0, 1), (2, 0), (3, 1), (1, 1), (2, 1))[n]
        at = col(dy, dz, 1)
        arrived(at, q, 0, parts[q], ksem, n)
        multiply(q, at)

    def row_ready():
        @pl.when(moves)
        def _():
            pl.semaphore_signal(ready, inc=1, device_id=(origin, c), device_id_type=MESH)

    def target_ready():
        @pl.when(moves)
        def _():
            pl.semaphore_wait(ready, 1)

    def step1(q, o):
        to = lax.rem(c + o, COLS)
        return pltpu.make_async_remote_copy(
            src_ref=ladder[q].at[group_at(r, to)], dst_ref=recv1[q].at[c], send_sem=s1_send.at[q, to], recv_sem=s1_recv.at[q, c],
            device_id=(r, to), device_id_type=MESH,
        )

    def exchange1(q):
        piece = pieces[q]

        def natural(n):
            group, rest = n // piece, n % piece
            return (rest // 4) * NOCC + group * 4 + rest % 4

        turned = lax.dot_general(
            one_hot((parts[q], parts[q]), natural), total[q][...].astype(jnp.bfloat16),
            (((1,), (1,)), ((), ())), preferred_element_type=jnp.float32,
        )
        ladder[q][...] = turned.astype(jnp.bfloat16).reshape(COLS, piece, width)

        def send(o, carry):
            step1(q, o).start()
            return carry

        lax.fori_loop(1, COLS, send, 0)
        recv1[q][c] = ladder[q][group_at(r, c)]

    def step2(q, to, slot):
        return pltpu.make_async_remote_copy(
            src_ref=send2[q].at[to], dst_ref=recv2[q].at[slot], send_sem=s2_send.at[q, to], recv_sem=s2_recv.at[q, slot],
            device_id=(target, to), device_id_type=MESH,
        )

    mine = r * 2 + k

    def exchange2(q):
        def arrive(o, carry):
            at = lax.rem(c + o, COLS)
            pltpu.make_async_remote_copy(
                src_ref=ladder[q].at[at], dst_ref=recv1[q].at[at], send_sem=s1_send.at[q, at], recv_sem=s1_recv.at[q, at],
                device_id=(r, at), device_id_type=MESH,
            ).wait_recv()
            return carry

        lax.fori_loop(1, COLS, arrive, 0)

        def send(o, carry):
            to = lax.rem(c + o, COLS)
            for b in range(BPC):
                source = partner[to * BPC + b] // BPC
                send2[q][to, :, b * BW : (b + 1) * BW] = recv1[q][source, :, b * BW : (b + 1) * BW]

            local = jnp.logical_and(target == r, to == c)

            @pl.when(jnp.logical_not(local))
            def _():
                step2(q, to, mine).start()

            @pl.when(local)
            def _():
                recv2[q][mine] = send2[q][to]

            return carry

        lax.fori_loop(0, COLS, send, 0)

    def exchange2_done(q):
        def arrive(slot, carry):
            there, column = sender(r, slot)

            @pl.when(jnp.logical_or(there != r, column != c))
            def _():
                step2(q, c, slot).wait_recv()

            return carry

        lax.fori_loop(0, 2 * ROWS, arrive, 0)

    send_own(0)
    lax.fori_loop(0, COLS, start_int, 0)
    lax.fori_loop(0, COLS, mask_ints, 0)
    multiply(0, c, first=True)
    near(0)
    over(0)
    send_own(1)
    near_twin(0)
    multiply(1, c, first=True)
    from_twin(0, 0)
    multiply(0, col(3, 0, 0))
    multiply(0, col(1, 0, 0))
    multiply(0, col(0, 1, 0))
    from_twin(0, 1)
    near_over(0)
    far(0)
    from_twin(0, 2)
    from_twin(0, 3)
    near(1)
    over(1)
    near_twin(1)
    near_over_twin(0)
    multiply(0, col(2, 0, 0))
    from_twin(0, 4)
    multiply(0, col(3, 1, 0))
    multiply(0, col(1, 1, 0))
    far_over(0)
    from_twin(0, 5)
    from_twin(0, 6)
    multiply(0, col(2, 1, 0))
    from_twin(0, 7)
    row_ready()
    exchange1(0)
    from_twin(1, 0)
    multiply(1, col(3, 0, 0))
    multiply(1, col(1, 0, 0))
    near_over(1)
    multiply(1, col(0, 1, 0))
    far(1)
    from_twin(1, 1)
    from_twin(1, 2)
    from_twin(1, 3)
    target_ready()
    exchange2(0)
    near_over_twin(1)
    multiply(1, col(2, 0, 0))
    from_twin(1, 4)
    multiply(1, col(3, 1, 0))
    multiply(1, col(1, 1, 0))
    far_over(1)
    from_twin(1, 5)
    from_twin(1, 6)
    multiply(1, col(2, 1, 0))
    from_twin(1, 7)
    exchange1(1)
    exchange2(1)
    exchange2_done(0)
    exchange2_done(1)
    for q in range(CHUNKS):
        piece = pieces[q]

        def grouped(m):
            first, second = m // NOCC, m % NOCC
            return (second // 4) * piece + first * 4 + second % 4

        result = jnp.dot(
            one_hot((parts[q], parts[q]), grouped), ladder[q][...].reshape(parts[q], width), preferred_element_type=jnp.float32
        )
        for p in range(CHUNKS):
            row = lax.broadcasted_iota(jnp.int32, (parts[q], parts[p]), 0)
            column = lax.broadcasted_iota(jnp.int32, (parts[q], parts[p]), 1)
            slot, rest = column // pieces[p], column % pieces[p]
            first = (slot % 2) * 4 + rest % 4
            second = (slot // 2) * ROWS + begins[p] // NOCC + rest // 4
            fetch = jnp.where(first * NOCC + second == row + begins[q], 1.0, 0.0).astype(jnp.bfloat16)
            result += jnp.dot(fetch, recv2[p][...].reshape(parts[p], width), preferred_element_type=jnp.float32)
        out_ref[begins[q] : begins[q] + parts[q], :] = (result * live).astype(jnp.bfloat16)

    for copy in started:
        copy.wait_send()
    for q in range(CHUNKS):

        def sent1(o, carry):
            step1(q, o).wait_send()
            return carry

        lax.fori_loop(1, COLS, sent1, 0)

        def sent2(to, carry):
            @pl.when(jnp.logical_not(jnp.logical_and(target == r, to == c)))
            def _():
                step2(q, to, mine).wait_send()

            return carry

        lax.fori_loop(0, COLS, sent2, 0)


def body(amplitudes, integrals, block_irrep, irrep_size, partner):
    rows, width = amplitudes.shape
    dma = pltpu.SemaphoreType.DMA
    held = [pltpu.VMEM((COLS, f * NOCC // COLS, width), jnp.bfloat16) for f in FIRSTS]
    return pl.pallas_call(
        kernel,
        out_shape=pltpu.VMEM((rows, width), jnp.bfloat16),
        in_specs=[pl.BlockSpec(memory_space=pltpu.SMEM)] * 3 + [pl.BlockSpec(memory_space=pl.ANY)] * 2,
        out_specs=pl.BlockSpec(memory_space=pltpu.VMEM),
        scratch_shapes=[
            pltpu.VMEM((COLS, rows, width), jnp.bfloat16),
            pltpu.VMEM((COLS, width, width), jnp.bfloat16),
            dma,
            dma((COLS,)),
            dma((CHUNKS, 12)),
            dma((CHUNKS, 12)),
            dma((CHUNKS, 8)),
            dma((CHUNKS, 8)),
            dma((CHUNKS, COLS)),
            dma((CHUNKS, COLS)),
            dma((CHUNKS, COLS)),
            dma((CHUNKS, COLS)),
            pltpu.SemaphoreType.REGULAR,
        ]
        + [pltpu.VMEM((width, f * NOCC), jnp.float32) for f in FIRSTS]
        + held * 4,
        compiler_params=pltpu.CompilerParams(
            collective_id=0, has_side_effects=True, vmem_limit_bytes=57 * 2**20
        ),
        name="ladder",
    )(block_irrep, irrep_size, partner, amplitudes, integrals)


def solution(mesh):
    in_specs = (P("row", "col"), P("col", None), P(), P(), P())
    return jax.shard_map(body, mesh=mesh, in_specs=in_specs, out_specs=P("row", "col"), check_vma=False)
```

```python
import jax
import jax.numpy as jnp
from jax import lax
from jax.experimental import pallas as pl
from jax.experimental.pallas import tpu as pltpu
from jax.sharding import PartitionSpec as P

MESH = pl.DeviceIdType.MESH
BW = 256
BPC = 4
NOCC = 64
COLS = 16
ROWS = 8
FIRSTS = (4, 4)
CHUNKS = len(FIRSTS)


def one_hot(shape, target):
    row = lax.broadcasted_iota(jnp.int32, shape, 0)
    column = lax.broadcasted_iota(jnp.int32, shape, 1)
    return jnp.where(column == target(row), 1.0, 0.0).astype(jnp.bfloat16)


def kernel(irrep, size, partner, amp_hbm, int_hbm, out_ref, *scratch):
    (amp, ints, own_sem, int_sem, y_send, y_recv, k_send, k_recv, s1_send, s1_recv, s2_send, s2_recv, ready) = scratch[:13]
    total, ladder, recv1, send2, recv2 = (scratch[13 + n * CHUNKS : 13 + (n + 1) * CHUNKS] for n in range(5))
    partial, ones = scratch[13 + 5 * CHUNKS : 13 + 6 * CHUNKS], scratch[13 + 6 * CHUNKS :]
    rows, width = amp_hbm.shape
    parts = [f * NOCC for f in FIRSTS]
    begins = [sum(parts[:q]) for q in range(CHUNKS)]
    pieces = [p // COLS for p in parts]
    r, c = lax.axis_index("row"), lax.axis_index("col")
    y, zh, k = c // 4, (c // 2) % 2, c % 2

    def col(dy, dz, dk):
        return lax.rem(y + dy, 4) * 4 + lax.rem(zh + dz, 2) * 2 + lax.rem(k + dk, 2)

    up, down, across, twin = (r, col(1, 0, 0)), (r, col(3, 0, 0)), (r, col(0, 1, 0)), (r, col(0, 0, 1))

    def group_at(row, s):
        sy, sz, sk = s // 4, (s // 2) % 2, s % 2
        x, z = lax.rem(row % 4 + sy + 2 * sk, 4), lax.rem(row // 4 + sz, 2)
        return (z * 4 + x) * 2 + sk

    def sender(row, slot):
        there, sk = slot // 2, slot % 2
        sz = lax.rem(row // 4 + there // 4, 2)
        sy = lax.rem(row % 4 + 8 - there % 4 - 2 * sk, 4)
        return there, sy * 4 + sz * 2 + sk

    target = group_at(r, c) // 2
    origin = lax.rem(r // 4 + zh, 2) * 4 + lax.rem(r % 4 + 8 - y - 2 * k, 4)
    moves = target != r

    own_copy = pltpu.make_async_copy(amp_hbm, amp.at[c], own_sem)
    own_copy.start()

    barrier = pltpu.get_barrier_semaphore()
    for to in (up, down, across, twin):
        pl.semaphore_signal(barrier, inc=1, device_id=to, device_id_type=MESH)

    @pl.when(moves)
    def _():
        pl.semaphore_signal(barrier, inc=1, device_id=(target, c), device_id_type=MESH)

    def int_copy(n):
        at = lax.rem(c + n, COLS)
        return pltpu.make_async_copy(
            int_hbm.at[:, pl.ds(pl.multiple_of(at * width, width), width)], ints.at[at], int_sem.at[at]
        )

    def live_of(base):
        lane = lax.broadcasted_iota(jnp.int32, (1, BW), 1)
        return jnp.concatenate(
            [jnp.where(lane < size[irrep[base + b]], 1.0, 0.0) for b in range(BPC)], axis=1
        )

    live = live_of(c * BPC)

    own_copy.wait()
    amp[c] *= live.astype(jnp.bfloat16)

    def start_int(n, carry):
        int_copy(n).start()
        return carry

    pl.semaphore_wait(barrier, jnp.where(moves, 5, 4))

    def move(at, q, start, count, to, sems, n):
        span = pl.ds(begins[q] + start, count)
        return pltpu.make_async_remote_copy(
            src_ref=amp.at[at, span], dst_ref=amp.at[at, span],
            send_sem=sems[0].at[q, n], recv_sem=sems[1].at[q, n],
            device_id=to, device_id_type=MESH,
        )

    ysem, ksem = (y_send, y_recv), (k_send, k_recv)
    started = []

    def go(copy):
        copy.start()
        started.append(copy)

    def send_own(q):
        go(move(c, q, 0, parts[q], up, ysem, 0))
        go(move(c, q, 0, parts[q], down, ysem, 1))
        go(move(c, q, 0, parts[q], across, ysem, 4))
        go(move(c, q, 0, parts[q], twin, ksem, 0))

    def arrived(at, q, start, count, sems, n):
        move(at, q, start, count, up, sems, n).wait_recv()

    def near(q):
        half = parts[q] // 2
        at = col(3, 0, 0)
        arrived(at, q, 0, parts[q], ysem, 0)
        go(move(at, q, 0, half, up, ysem, 2))
        go(move(at, q, half, half, across, ysem, 7))
        at = col(1, 0, 0)
        arrived(at, q, 0, parts[q], ysem, 1)
        go(move(at, q, half, half, down, ysem, 3))
        go(move(at, q, 0, half, across, ysem, 8))

    def near_twin(q):
        go(move(col(3, 0, 0), q, 0, parts[q], twin, ksem, 1))
        go(move(col(1, 0, 0), q, 0, parts[q], twin, ksem, 2))

    def over(q):
        half = parts[q] // 2
        at = col(0, 1, 0)
        arrived(at, q, 0, parts[q], ysem, 4)
        go(move(at, q, 0, half, up, ysem, 5))
        go(move(at, q, half, half, down, ysem, 6))
        go(move(at, q, 0, parts[q], twin, ksem, 3))

    def edge(q):
        return parts[q] * 5 // 16

    def far(q):
        half = parts[q] // 2
        at = col(2, 0, 0)
        arrived(at, q, 0, half, ysem, 2)
        arrived(at, q, half, half, ysem, 3)
        go(move(at, q, edge(q), parts[q] - 2 * edge(q), across, ysem, 11))
        go(move(at, q, 0, parts[q], twin, ksem, 4))

    def near_over(q):
        half = parts[q] // 2
        at = col(3, 1, 0)
        arrived(at, q, 0, half, ysem, 5)
        go(move(at, q, 0, edge(q), up, ysem, 9))
        at = col(1, 1, 0)
        arrived(at, q, half, half, ysem, 6)
        go(move(at, q, parts[q] - edge(q), edge(q), down, ysem, 10))

    def near_over_twin(q):
        half = parts[q] // 2
        at = col(3, 1, 0)
        arrived(at, q, half, half, ysem, 7)
        go(move(at, q, 0, parts[q], twin, ksem, 5))
        at = col(1, 1, 0)
        arrived(at, q, 0, half, ysem, 8)
        go(move(at, q, 0, parts[q], twin, ksem, 6))

    def far_over(q):
        at = col(2, 1, 0)
        arrived(at, q, 0, edge(q), ysem, 9)
        arrived(at, q, parts[q] - edge(q), edge(q), ysem, 10)
        arrived(at, q, edge(q), parts[q] - 2 * edge(q), ysem, 11)
        go(move(at, q, 0, parts[q], twin, ksem, 7))

    def mask_ints(n, carry):
        int_copy(n).wait()
        at = lax.rem(c + n, COLS)
        for a in range(BPC):
            for b in range(BPC):
                same = irrep[c * BPC + a] == irrep[at * BPC + b]
                keep = jnp.where(same, 1.0, 0.0).astype(jnp.bfloat16)
                ints[at, a * BW : (a + 1) * BW, b * BW : (b + 1) * BW] *= keep
        return carry

    def multiply(q, at, first=False):
        product = lax.dot_general(
            ints[at], amp[at, begins[q] : begins[q] + parts[q], :],
            (((1,), (1,)), ((), ())), preferred_element_type=jnp.float32,
        )
        total[q][...] = product if first else total[q][...] + product

    def from_twin(q, n):
        dy, dz = ((0, 0), (3, 0), (1, 0), (0, 1), (2, 0), (3, 1), (1, 1), (2, 1))[n]
        at = col(dy, dz, 1)
        arrived(at, q, 0, parts[q], ksem, n)
        multiply(q, at)

    def row_ready():
        @pl.when(moves)
        def _():
            pl.semaphore_signal(ready, inc=1, device_id=(origin, c), device_id_type=MESH)

    def target_ready():
        @pl.when(moves)
        def _():
            pl.semaphore_wait(ready, 1)

    def step1(q, o):
        to = lax.rem(c + o, COLS)
        return pltpu.make_async_remote_copy(
            src_ref=ladder[q].at[group_at(r, to)], dst_ref=recv1[q].at[c], send_sem=s1_send.at[q, to], recv_sem=s1_recv.at[q, c],
            device_id=(r, to), device_id_type=MESH,
        )

    def exchange1(q):
        piece = pieces[q]

        def natural(n):
            group, rest = n // piece, n % piece
            return (rest // 4) * NOCC + group * 4 + rest % 4

        turned = lax.dot_general(
            one_hot((parts[q], parts[q]), natural), total[q][...].astype(jnp.bfloat16),
            (((1,), (1,)), ((), ())), preferred_element_type=jnp.float32,
        )
        ladder[q][...] = turned.astype(jnp.bfloat16).reshape(COLS, piece, width)

        def send(o, carry):
            step1(q, o).start()
            return carry

        lax.fori_loop(1, COLS, send, 0)
        recv1[q][c] = ladder[q][group_at(r, c)]

    def step2(q, to, slot):
        return pltpu.make_async_remote_copy(
            src_ref=send2[q].at[to], dst_ref=recv2[q].at[slot], send_sem=s2_send.at[q, to], recv_sem=s2_recv.at[q, slot],
            device_id=(target, to), device_id_type=MESH,
        )

    mine = r * 2 + k

    def exchange2(q):
        def arrive(o, carry):
            at = lax.rem(c + o, COLS)
            pltpu.make_async_remote_copy(
                src_ref=ladder[q].at[at], dst_ref=recv1[q].at[at], send_sem=s1_send.at[q, at], recv_sem=s1_recv.at[q, at],
                device_id=(r, at), device_id_type=MESH,
            ).wait_recv()
            return carry

        lax.fori_loop(1, COLS, arrive, 0)

        def send(o, carry):
            to = lax.rem(c + o, COLS)
            for b in range(BPC):
                source = partner[to * BPC + b] // BPC
                send2[q][to, :, b * BW : (b + 1) * BW] = recv1[q][source, :, b * BW : (b + 1) * BW]

            local = jnp.logical_and(target == r, to == c)

            @pl.when(jnp.logical_not(local))
            def _():
                step2(q, to, mine).start()

            @pl.when(local)
            def _():
                recv2[q][mine] = send2[q][to]

            return carry

        lax.fori_loop(0, COLS, send, 0)

    def exchange2_done(q):
        def arrive(slot, carry):
            there, column = sender(r, slot)

            @pl.when(jnp.logical_or(there != r, column != c))
            def _():
                step2(q, c, slot).wait_recv()

            return carry

        lax.fori_loop(0, 2 * ROWS, arrive, 0)

    send_own(0)
    lax.fori_loop(0, COLS, start_int, 0)
    lax.fori_loop(0, COLS, mask_ints, 0)
    multiply(0, c, first=True)
    near(0)
    over(0)
    send_own(1)
    near_twin(0)
    multiply(1, c, first=True)
    from_twin(0, 0)
    multiply(0, col(3, 0, 0))
    multiply(0, col(1, 0, 0))
    multiply(0, col(0, 1, 0))
    from_twin(0, 1)
    far(0)
    near_over(0)
    from_twin(0, 2)
    from_twin(0, 3)
    near(1)
    over(1)
    near_twin(1)
    near_over_twin(0)
    multiply(0, col(2, 0, 0))
    from_twin(0, 4)
    multiply(0, col(3, 1, 0))
    multiply(0, col(1, 1, 0))
    far_over(0)
    from_twin(0, 5)
    from_twin(0, 6)
    multiply(0, col(2, 1, 0))
    from_twin(0, 7)
    row_ready()
    exchange1(0)
    from_twin(1, 0)
    multiply(1, col(3, 0, 0))
    multiply(1, col(1, 0, 0))
    near_over(1)
    far(1)
    multiply(1, col(0, 1, 0))
    from_twin(1, 1)
    from_twin(1, 2)
    from_twin(1, 3)
    target_ready()
    exchange2(0)
    near_over_twin(1)
    multiply(1, col(2, 0, 0))
    from_twin(1, 4)
    multiply(1, col(3, 1, 0))
    multiply(1, col(1, 1, 0))
    far_over(1)
    from_twin(1, 5)
    from_twin(1, 6)
    multiply(1, col(2, 1, 0))
    from_twin(1, 7)
    exchange1(1)
    exchange2(1)
    def fetch(q, p):
        row = lax.broadcasted_iota(jnp.int32, (parts[q], parts[p]), 0)
        column = lax.broadcasted_iota(jnp.int32, (parts[q], parts[p]), 1)
        slot, rest = column // pieces[p], column % pieces[p]
        first = (slot % 2) * 4 + rest % 4
        second = (slot // 2) * ROWS + begins[p] // NOCC + rest // 4
        return jnp.where(first * NOCC + second == row + begins[q], 1.0, 0.0).astype(jnp.bfloat16)

    for q in range(CHUNKS):
        piece = pieces[q]

        def grouped(m):
            first, second = m // NOCC, m % NOCC
            return (second // 4) * piece + first * 4 + second % 4

        result = jnp.dot(
            one_hot((parts[q], parts[q]), grouped), ladder[q][...].reshape(parts[q], width), preferred_element_type=jnp.float32
        )
        if q == 0:
            exchange2_done(0)
        partial[q][...] = result + jnp.dot(
            fetch(q, 0), recv2[0][...].reshape(parts[0], width), preferred_element_type=jnp.float32
        )
        ones[q][...] = fetch(q, 1)
    exchange2_done(1)
    for q in range(CHUNKS):
        result = partial[q][...] + jnp.dot(
            ones[q][...], recv2[1][...].reshape(parts[1], width), preferred_element_type=jnp.float32
        )
        out_ref[begins[q] : begins[q] + parts[q], :] = (result * live).astype(jnp.bfloat16)

    for copy in started:
        copy.wait_send()
    for q in range(CHUNKS):

        def sent1(o, carry):
            step1(q, o).wait_send()
            return carry

        lax.fori_loop(1, COLS, sent1, 0)

        def sent2(to, carry):
            @pl.when(jnp.logical_not(jnp.logical_and(target == r, to == c)))
            def _():
                step2(q, to, mine).wait_send()

            return carry

        lax.fori_loop(0, COLS, sent2, 0)


def body(amplitudes, integrals, block_irrep, irrep_size, partner):
    rows, width = amplitudes.shape
    dma = pltpu.SemaphoreType.DMA
    held = [pltpu.VMEM((COLS, f * NOCC // COLS, width), jnp.bfloat16) for f in FIRSTS]
    return pl.pallas_call(
        kernel,
        out_shape=pltpu.VMEM((rows, width), jnp.bfloat16),
        in_specs=[pl.BlockSpec(memory_space=pltpu.SMEM)] * 3 + [pl.BlockSpec(memory_space=pl.ANY)] * 2,
        out_specs=pl.BlockSpec(memory_space=pltpu.VMEM),
        scratch_shapes=[
            pltpu.VMEM((COLS, rows, width), jnp.bfloat16),
            pltpu.VMEM((COLS, width, width), jnp.bfloat16),
            dma,
            dma((COLS,)),
            dma((CHUNKS, 12)),
            dma((CHUNKS, 12)),
            dma((CHUNKS, 8)),
            dma((CHUNKS, 8)),
            dma((CHUNKS, COLS)),
            dma((CHUNKS, COLS)),
            dma((CHUNKS, COLS)),
            dma((CHUNKS, COLS)),
            pltpu.SemaphoreType.REGULAR,
        ]
        + [pltpu.VMEM((width, f * NOCC), jnp.float32) for f in FIRSTS]
        + held * 4
        + [pltpu.VMEM((f * NOCC, width), jnp.float32) for f in FIRSTS]
        + [pltpu.VMEM((f * NOCC, FIRSTS[1] * NOCC), jnp.bfloat16) for f in FIRSTS],
        compiler_params=pltpu.CompilerParams(
            collective_id=0, has_side_effects=True, vmem_limit_bytes=59 * 2**20
        ),
        name="ladder",
    )(block_irrep, irrep_size, partner, amplitudes, integrals)


def solution(mesh):
    in_specs = (P("row", "col"), P("col", None), P(), P(), P())
    return jax.shard_map(body, mesh=mesh, in_specs=in_specs, out_specs=P("row", "col"), check_vma=False)
```
